128 devices in a mesh: heads: 8 (over z, core), tok: 16 (over y, x).
Axes of the slice: x: 4, y: 4, z: 4, core: 2. Of those that a mesh axis runs over, the one named last changes fastest.
Arguments:
- states: bfloat16 [512, 7168], P('heads', 'tok'), may hold values from -10 to 10
- key_values: bfloat16 [2, 2, 8192, 7168], P(None, None, 'tok', 'heads')
- cache_length: int32 [2], replicated, may hold values from 0 to 7936, as said below
- norm1_gain: float32 [7168], replicated, may hold values from 0.25 to 1.75
- norm1_bias: float32 [7168], replicated, may hold values from -3 to 3
- qkv_weight: bfloat16 [7168, 3, 7168], P('tok', None, 'heads'), may hold values from -0.0625 to 0.0625
- qkv_bias: float32 [3, 7168], P(None, 'heads'), may hold values from -3 to 3
- out_weight: bfloat16 [7168, 7168], P('heads', 'tok'), may hold values from -0.0625 to 0.0625
- out_bias: float32 [7168], P('tok'), may hold values from -3 to 3
- norm2_gain: float32 [7168], replicated, may hold values from 0.25 to 1.75
- norm2_bias: float32 [7168], replicated, may hold values from -3 to 3
- fc1_weight: bfloat16 [7168, 28672], P(None, ('heads', 'tok')), may hold values from -0.0625 to 0.0625
- fc1_bias: float32 [28672], P(('heads', 'tok')), may hold values from -3 to 3
- fc2_weight: bfloat16 [28672, 7168], P(('heads', 'tok')), may hold values from -0.03125 to 0.03125
- fc2_bias: float32 [7168], P('tok'), may hold values from -3 to 3
Outputs:
- hidden_out: bfloat16 [512, 7168], P('heads', 'tok')
- cache_out: bfloat16 [2, 2, 8192, 7168], P(None, None, 'tok', 'heads')
The draws below stay inside these ranges and needn't reach their ends.
Inputs may be any that keep to these rules, and one draw needn't show every extreme that they name: Request r's new tokens take positions cache_length[r] to cache_length[r] + 255 of its cache; some request reaches the largest length.
All inputs are finite; a program needn't handle non-finite values.
Results may differ from the reference program's by a relative error of at most 0.013.
The reference program's roundings to bfloat16 on the way count: a program that leaves them out, or rounds other values in their place, can miss the bound.
Values may be sent and summed in bfloat16 or wider, within the bound.
A program may use at most 192 MiB of HBM per device.

```python
import math
import jax
import jax.numpy as jnp
from jax import lax

D = 7168
HEADS = 56
FF = 28672
HD = 128
SINK = 4
REQS = 2
NEW = 256
CAP = 8192
WINDOW = 4096
TOKENS = 512


def draw_cache_length(key, part):
    first, second = jax.random.split(jax.random.fold_in(key, 11))
    others = jax.random.randint(first, (REQS,), 0, CAP - NEW + 1)
    fullest = jax.random.randint(second, (), 0, REQS)
    return jnp.where(jnp.arange(REQS) == fullest, CAP - NEW, others).astype(jnp.int32)


def draw_key_values(key, part):
    base_key = jax.random.fold_in(jax.random.fold_in(key, 23), 0)
    values = jax.random.normal(base_key, (2, REQS, CAP, D), jnp.float32)
    return values.astype(jnp.bfloat16)


def draw_states(key, part):
    base_key = jax.random.fold_in(key, 37)
    position = jnp.arange(D, dtype=jnp.float32) / (D - 1)
    scale = jnp.exp(math.log(0.25) + math.log(10.0) * position)
    values = jnp.clip(jax.random.normal(base_key, (TOKENS, D), jnp.float32), -4.0, 4.0)
    return (values * scale[None, :]).astype(jnp.bfloat16)


def levels(stream_key, dims, cuts, low, high):
    loudness = 1.0
    for axis_at, blocks in cuts:
        draws = jax.random.uniform(jax.random.fold_in(jax.random.fold_in(stream_key, 6), axis_at), (blocks,), jnp.float32, low / len(cuts), high / len(cuts))
        loudness = loudness * jnp.repeat(jnp.exp(draws), dims[axis_at] // blocks).reshape((-1,) + (1,) * (len(dims) - 1 - axis_at))
    return loudness


def centred(rng, extent, deviation, most, cuts=(), kind=jnp.bfloat16):
    result = jax.random.normal(rng, extent, jnp.float32) * deviation
    if len(cuts) > 0:
        result = levels(rng, extent, cuts, -0.22, 0.18) * result
    return jnp.clip(result, min=-most, max=most).astype(kind)


def setup_inputs(seed: int = 0) -> dict:
    key_list = jax.random.split(jax.random.key(seed), 16)
    states = draw_states(jax.random.fold_in(key_list[15], 71), 0)
    key_values = draw_key_values(jax.random.fold_in(key_list[15], 71), 0)
    cache_length = draw_cache_length(jax.random.fold_in(key_list[15], 71), 0)
    norm1_gain = jnp.clip(1.0 + 0.15 * jax.random.normal(key_list[3], (D,), jnp.float32), 0.25, 1.75)
    norm1_bias = centred(key_list[4], (D,), 0.5, 3.0, (), jnp.float32)
    qkv_weight = centred(key_list[5], (D, 3, D), D ** -0.5, 0.0625, ((0, 16), (2, 8)))
    qkv_bias = centred(key_list[6], (3, D), 0.5, 3.0, ((1, 8),), jnp.float32)
    out_weight = centred(key_list[7], (D, D), D ** -0.5, 0.0625, ((0, 8), (1, 16)))
    out_bias = centred(key_list[8], (D,), 0.5, 3.0, ((0, 16),), jnp.float32)
    norm2_gain = jnp.clip(1.0 + 0.15 * jax.random.normal(key_list[9], (D,), jnp.float32), 0.25, 1.75)
    norm2_bias = centred(key_list[10], (D,), 0.5, 3.0, (), jnp.float32)
    fc1_weight = centred(key_list[11], (D, FF), D ** -0.5, 0.0625, ((1, 128),))
    fc1_bias = centred(key_list[12], (FF,), 0.5, 3.0, ((0, 128),), jnp.float32)
    fc2_weight = centred(key_list[13], (FF, D), FF ** -0.5, 0.03125, ((0, 128),))
    fc2_bias = centred(key_list[14], (D,), 0.5, 3.0, ((0, 16),), jnp.float32)
    return {"states": states, "key_values": key_values, "cache_length": cache_length, "norm1_gain": norm1_gain, "norm1_bias": norm1_bias, "qkv_weight": qkv_weight, "qkv_bias": qkv_bias, "out_weight": out_weight, "out_bias": out_bias, "norm2_gain": norm2_gain, "norm2_bias": norm2_bias, "fc1_weight": fc1_weight, "fc1_bias": fc1_bias, "fc2_weight": fc2_weight, "fc2_bias": fc2_bias}


def layer_norm(values, gain, shift):
    values = values.astype(jnp.float32)
    mean_row = lax.optimization_barrier(jnp.mean(values, axis=-1, keepdims=True))
    variance = lax.optimization_barrier(jnp.mean((values - mean_row) ** 2, axis=-1, keepdims=True))
    return (values - mean_row) * lax.rsqrt(variance + 1e-05) * gain + shift

def reference(states, key_values, cache_length, norm1_gain, norm1_bias, qkv_weight, qkv_bias, out_weight, out_bias, norm2_gain, norm2_bias, fc1_weight, fc1_bias, fc2_weight, fc2_bias):
    normed1 = layer_norm(states, norm1_gain, norm1_bias).astype(jnp.bfloat16)
    summed = jnp.dot(normed1, qkv_weight.reshape(D, 3 * D), preferred_element_type=jnp.float32).reshape(TOKENS, 3, D)
    factors = jnp.asarray([HD ** (-0.5), 1.0, 1.0], dtype=jnp.float32)[None, :, None]
    projected = ((summed + qkv_bias[None]) * factors).astype(jnp.bfloat16)
    fresh = jnp.moveaxis(projected[:, 1:].reshape(REQS, NEW, 2, D), 2, 0)
    cache_out = key_values
    zero = jnp.int32(0)
    for request in range(REQS):
        cache_out = lax.dynamic_update_slice(cache_out, fresh[:, request:request + 1], (zero, jnp.int32(request), cache_length[request].astype(jnp.int32), zero))
    key_pos = jnp.arange(CAP, dtype=jnp.int32)
    outputs = []
    for request in range(REQS):
        query_pos = cache_length[request].astype(jnp.int32) + jnp.arange(NEW, dtype=jnp.int32)
        allowed = (key_pos[None, :] <= query_pos[:, None]) & ((key_pos[None, :] < SINK) | (query_pos[:, None] - key_pos[None, :] < WINDOW))
        queries = projected[request * NEW:(request + 1) * NEW, 0].reshape(NEW, HEADS, HD).transpose(1, 0, 2)
        keys = cache_out[0, request].reshape(CAP, HEADS, HD).transpose(1, 0, 2)
        values = cache_out[1, request].reshape(CAP, HEADS, HD).transpose(1, 0, 2)

        def one_head(operands):
            query_h, key_h, value_h = operands
            scores = jnp.dot(query_h, key_h.T, preferred_element_type=jnp.float32)
            masked = jnp.where(allowed, scores, -1e+30)
            peak = lax.optimization_barrier(jnp.max(masked, axis=-1, keepdims=True))
            weights = jnp.where(allowed, jnp.exp(masked - peak), 0.0)
            totals = lax.optimization_barrier(jnp.sum(weights, axis=-1, keepdims=True))
            return jnp.dot(weights.astype(jnp.bfloat16), value_h, preferred_element_type=jnp.float32) / totals
        heads_out = lax.map(one_head, (queries, keys, values))
        outputs.append(heads_out.transpose(1, 0, 2).reshape(NEW, D))
    attended = jnp.concatenate(outputs, axis=0).astype(jnp.bfloat16)
    residual = (states.astype(jnp.float32) + jnp.dot(attended, out_weight, preferred_element_type=jnp.float32) + out_bias).astype(jnp.bfloat16)
    normed2 = layer_norm(residual, norm2_gain, norm2_bias).astype(jnp.bfloat16)
    active = jnp.maximum(jnp.dot(normed2, fc1_weight, preferred_element_type=jnp.float32) + fc1_bias, 0.0).astype(jnp.bfloat16)
    hidden_out = (residual.astype(jnp.float32) + jnp.dot(active, fc2_weight, preferred_element_type=jnp.float32) + fc2_bias).astype(jnp.bfloat16)
    return (hidden_out, cache_out)
```

```python
import jax
import jax.numpy as jnp
from jax import lax
from jax.sharding import PartitionSpec as P

HD = 128
SINK = 4
REQS = 2
NEW = 256


EPSILON = 1e-05
NEGATIVE = -1e30


def norm_rows(values, total_sum, total_square, width, gain, shift):
    mean_row = total_sum / width
    variance = total_square / width - mean_row * mean_row
    return (
        (values - mean_row[:, None]) * lax.rsqrt(variance[:, None] + EPSILON) * gain + shift
    ).astype(jnp.bfloat16)


def shards(
    states,
    key_values,
    cache_length,
    norm1_gain,
    norm1_bias,
    qkv_weight,
    qkv_bias,
    out_weight,
    out_bias,
    norm2_gain,
    norm2_bias,
    fc1_weight,
    fc1_bias,
    fc2_weight,
    fc2_bias,
):
    head_count = lax.axis_size("heads")
    tok_count = lax.axis_size("tok")
    tok_index = lax.axis_index("tok")
    rows_local, cols_local = states.shape
    width = cols_local * tok_count
    group = qkv_weight.shape[2]
    group_heads = group // HD
    tokens = rows_local * head_count
    cache_rows = key_values.shape[2]
    window = cache_rows * tok_count // 2
    col_start = tok_index * cols_local
    states_float = states.astype(jnp.float32)
    row_sum, row_square = lax.psum(
        (jnp.sum(states_float, axis=1), jnp.sum(states_float * states_float, axis=1)), "tok"
    )
    gain_one = lax.dynamic_slice_in_dim(norm1_gain, col_start, cols_local)
    shift_one = lax.dynamic_slice_in_dim(norm1_bias, col_start, cols_local)
    normed_one = norm_rows(states_float, row_sum, row_square, width, gain_one, shift_one)
    gathered = lax.all_gather(normed_one, "heads", axis=0, tiled=True)
    weight_flat = qkv_weight.reshape(cols_local, 3 * group)
    factors = jnp.asarray([HD ** (-0.5), 1.0, 1.0], dtype=jnp.float32)[None, :, None]
    partial_qkv = jnp.dot(gathered, weight_flat, preferred_element_type=jnp.float32)
    summed = lax.psum_scatter(partial_qkv, "tok", scatter_dimension=0, tiled=True)
    projected_part = ((summed.reshape(-1, 3, group) + qkv_bias[None]) * factors).astype(jnp.bfloat16)
    projected = lax.all_gather(projected_part, "tok", axis=0, tiled=True)
    queries = projected[:, 0].reshape(REQS, NEW, group_heads, HD)
    fresh = jnp.moveaxis(projected[:, 1:].reshape(REQS, NEW, 2, group), 2, 0)
    key_pos = tok_index * cache_rows + jnp.arange(cache_rows, dtype=jnp.int32)
    appended_parts = []
    for request in range(REQS):
        offset = key_pos - cache_length[request]
        inside = (offset >= 0) & (offset < NEW)
        picked = jnp.take(fresh[:, request], jnp.clip(offset, 0, NEW - 1), axis=1)
        appended_parts.append(jnp.where(inside[None, :, None], picked, key_values[:, request]))
    appended = jnp.stack(appended_parts, axis=1)
    keys = appended[0].reshape(REQS, cache_rows, group_heads, HD)
    values = appended[1].reshape(REQS, cache_rows, group_heads, HD)
    query_pos = cache_length[:, None] + jnp.arange(NEW, dtype=jnp.int32)[None, :]
    distance = query_pos[:, :, None] - key_pos[None, None, :]
    allowed = (distance >= 0) & ((key_pos[None, None, :] < SINK) | (distance < window))
    scores = jnp.einsum("rshd,rphd->rshp", queries, keys, preferred_element_type=jnp.float32)
    masked = jnp.where(allowed[:, :, None, :], scores, NEGATIVE)
    peak = lax.pmax(jnp.max(masked, axis=-1), "tok")
    weights = jnp.where(allowed[:, :, None, :], jnp.exp(masked - peak[..., None]), 0.0)
    totals = jnp.sum(weights, axis=-1)
    partial_out = jnp.einsum(
        "rshp,rphd->rshd", weights.astype(jnp.bfloat16), values, preferred_element_type=jnp.float32
    )
    merged = lax.psum_scatter(partial_out.reshape(tokens, group), "tok", scatter_dimension=0, tiled=True)
    denominator = lax.psum_scatter(totals.reshape(tokens, group_heads), "tok", scatter_dimension=0, tiled=True)
    attended_part = (
        (merged.reshape(-1, group_heads, HD) / denominator[..., None]).astype(jnp.bfloat16).reshape(-1, group)
    )
    attended = lax.all_gather(attended_part, "tok", axis=0, tiled=True)
    projected_out = lax.psum_scatter(
        jnp.dot(attended, out_weight, preferred_element_type=jnp.float32),
        "heads",
        scatter_dimension=0,
        tiled=True,
    )
    residual = (states_float + projected_out + out_bias).astype(jnp.bfloat16)
    residual_float = residual.astype(jnp.float32)
    second_sum, second_square = lax.psum(
        (jnp.sum(residual_float, axis=1), jnp.sum(residual_float * residual_float, axis=1)), "tok"
    )
    gain_two = lax.dynamic_slice_in_dim(norm2_gain, col_start, cols_local)
    shift_two = lax.dynamic_slice_in_dim(norm2_bias, col_start, cols_local)
    normed_part = norm_rows(residual_float, second_sum, second_square, width, gain_two, shift_two)
    normed = lax.all_gather(normed_part, "tok", axis=1, tiled=True)
    active = jnp.maximum(
        jnp.dot(
            lax.all_gather(normed, "heads", axis=0, tiled=True),
            fc1_weight,
            preferred_element_type=jnp.float32,
        )
        + fc1_bias,
        0.0,
    ).astype(jnp.bfloat16)
    hidden_local = fc1_weight.shape[1]
    term = jnp.einsum(
        "hnf,ftc->htnc",
        active.reshape(head_count, rows_local, hidden_local),
        fc2_weight.reshape(hidden_local, tok_count, cols_local),
        preferred_element_type=jnp.float32,
    )
    pieces = lax.all_to_all(
        term.reshape(head_count * tok_count, rows_local, cols_local).astype(jnp.bfloat16),
        ("heads", "tok"),
        0,
        0,
        tiled=True,
    )
    down = jnp.sum(pieces.astype(jnp.float32), axis=0)
    hidden_out = (residual_float + down + fc2_bias).astype(jnp.bfloat16)
    return (hidden_out, appended)


def solution(mesh):
    placed = (
        P("heads", "tok"),
        P(None, None, "tok", "heads"),
        P(),
        P(),
        P(),
        P("tok", None, "heads"),
        P(None, "heads"),
        P("heads", "tok"),
        P("tok"),
        P(),
        P(),
        P(None, ("heads", "tok")),
        P(("heads", "tok")),
        P(("heads", "tok"), None),
        P("tok"),
    )
    return jax.shard_map(
        shards,
        mesh=mesh,
        in_specs=placed,
        out_specs=(P("heads", "tok"), P(None, None, "tok", "heads")),
        check_vma=False,
    )
```
